1024 devices in a mesh: seq: 32 (over y, z_hi, core), chan: 32 (over x, z_lo).
Axes of the slice: x: 4, y: 8, z: 16 (z_hi: 2, z_lo: 8; z = z_hi * 8 + z_lo), core: 2. Of those that a mesh axis runs over, the one named last changes fastest.
Arguments:
- query_rows: bfloat16 [4096, 8192], P('seq', 'chan'), may hold values from -6 to 6
- key_rows: bfloat16 [4096, 8192], P('seq', 'chan'), may hold values from -6 to 6
- value_rows: bfloat16 [4096, 8192], P('seq', 'chan'), may hold values from -6 to 6
- short_taps: float32 [3, 3, 8192], P(None, None, 'chan'), may hold values from -3.5 to 3.5
- long_filter: float32 [4096, 128], P('seq'), may hold values from -1.1 to 1.1
- cotangent: bfloat16 [4096, 8192], P('seq', 'chan'), may hold values from -6 to 6
Outputs:
- hyena_out: bfloat16 [4096, 8192], P('seq', 'chan')
- grad_query: bfloat16 [4096, 8192], P('seq', 'chan')
- grad_key: bfloat16 [4096, 8192], P('seq', 'chan')
- grad_value: bfloat16 [4096, 8192], P('seq', 'chan')
- grad_filter: float32 [4096, 128], P('seq')
The draws below stay inside these ranges and needn't reach their ends.
All inputs are finite; a program needn't handle non-finite values.
Results may differ from the reference program's by a relative error of at most 0.001.
Values may be sent and summed in bfloat16 or wider, within the bound.
A program may use at most 32 MiB of HBM per device.

```python
import math
import jax
import jax.numpy as jnp
from jax import lax

D = 8192
FILTER_GROUPS = 128
KS = 3
TOKEN_LENGTH = 4096


def draw_long_filter(key, part):
    random_subkeys = jax.random.split(key, 5)
    position = jnp.arange(TOKEN_LENGTH, dtype=jnp.float32)[:, None]
    slow_share = 0.5
    slow_pick = jax.random.uniform(random_subkeys[0], (FILTER_GROUPS,)) < slow_share
    slow_scale = jnp.exp(jax.random.uniform(random_subkeys[1], (FILTER_GROUPS,), minval=math.log(0.5 * TOKEN_LENGTH), maxval=math.log(4.0 * TOKEN_LENGTH)))
    fast_scale = jax.random.uniform(random_subkeys[2], (FILTER_GROUPS,), minval=30.0, maxval=50.0)
    horizon = jnp.where(slow_pick, slow_scale, fast_scale)
    spike_position = jax.random.randint(random_subkeys[3], (4, FILTER_GROUPS), 0, TOKEN_LENGTH)
    steps_elapsed = jnp.arange(TOKEN_LENGTH, dtype=jnp.int32)[None, :, None] >= spike_position[:, None, :]
    spike_events = jnp.sum(steps_elapsed.astype(jnp.float32), axis=0)
    survival_fraction = jnp.exp(spike_events * math.log(0.6))
    jitter = jax.random.truncated_normal(random_subkeys[4], -4.0, 4.0, (TOKEN_LENGTH, FILTER_GROUPS))
    amplitude = 1.0 / jnp.sqrt(0.5 * jnp.minimum(horizon, float(TOKEN_LENGTH)))
    return (jitter * jnp.exp(-position / horizon) * survival_fraction * amplitude).astype(jnp.float32)


def steps_of(key, extent, cuts, smallest, high):
    gain, own = 1.0, jax.random.fold_in(key, 6)
    for dim, shards_of in cuts:
        draws = jnp.exp(jax.random.uniform(jax.random.fold_in(own, dim), (shards_of,), jnp.float32, smallest / len(cuts), high / len(cuts)))
        gain = gain * jnp.repeat(draws, extent[dim] // shards_of).reshape([-1 if axis == dim else 1 for axis in range(len(extent))])
    return gain


def bell_draw(own_key, dims, deviation, most, pieces=(), kind=jnp.bfloat16):
    entries = deviation * jax.random.normal(own_key, dims, jnp.float32)
    if pieces:
        entries = entries * steps_of(own_key, dims, pieces, -0.22, 0.18)
    return jnp.clip(entries, -most, most).astype(kind)


def setup_inputs(seed: int = 0) -> dict:
    splits = jax.random.split(jax.random.key(seed), 7)
    query_rows = bell_draw(splits[0], (TOKEN_LENGTH, D), 1.0, 6.0, ((0, 32), (1, 32)))
    key_rows = bell_draw(splits[1], (TOKEN_LENGTH, D), 1.0, 6.0, ((0, 32), (1, 32)))
    value_rows = bell_draw(splits[2], (TOKEN_LENGTH, D), 1.0, 6.0, ((0, 32), (1, 32)))
    short_taps = bell_draw(splits[3], (3, KS, D), KS ** -0.5, 3.5, ((2, 32),), jnp.float32)
    long_filter = draw_long_filter(jax.random.fold_in(splits[6], 71), 0)
    cotangent = bell_draw(splits[5], (TOKEN_LENGTH, D), 1.0, 6.0, ((0, 32), (1, 32)))
    return {"query_rows": query_rows, "key_rows": key_rows, "value_rows": value_rows, "short_taps": short_taps, "long_filter": long_filter, "cotangent": cotangent}


def causal_taps(signal, tap_weights):
    summed = tap_weights[0] * signal
    for shift_by in range(1, tap_weights.shape[0]):
        delayed = jnp.concatenate([jnp.zeros((shift_by, signal.shape[1]), signal.dtype), signal[:-shift_by]], axis=0)
        summed = summed + tap_weights[shift_by] * delayed
    return summed


def anticausal_taps(signal, tap_weights):
    summed = tap_weights[0] * signal
    for shift_by in range(1, tap_weights.shape[0]):
        advanced = jnp.concatenate([signal[shift_by:], jnp.zeros((shift_by, signal.shape[1]), signal.dtype)], axis=0)
        summed = summed + tap_weights[shift_by] * advanced
    return summed


def reference(query_rows, key_rows, value_rows, short_taps, long_filter, cotangent):
    width_block = math.gcd(D, FILTER_GROUPS * max(1, 1024 // FILTER_GROUPS))
    block_count = D // width_block
    padded_len = 2 * TOKEN_LENGTH

    def one_block(filter_sum, block_id):
        first_col = block_id * width_block

        def columns_of(source):
            return lax.dynamic_slice_in_dim(source, first_col, width_block, source.ndim - 1)

        taps_block = columns_of(short_taps)
        query_conv = causal_taps(columns_of(query_rows).astype(jnp.float32), taps_block[0])
        key_conv = causal_taps(columns_of(key_rows).astype(jnp.float32), taps_block[1])
        value_conv = causal_taps(columns_of(value_rows).astype(jnp.float32), taps_block[2])
        gated_rows = key_conv * value_conv
        filter_wide = jnp.tile(long_filter, (1, width_block // FILTER_GROUPS))
        gated_spec = jnp.fft.rfft(gated_rows, n=padded_len, axis=0)
        filter_spec = jnp.fft.rfft(filter_wide, n=padded_len, axis=0)
        long_conv = jnp.fft.irfft(gated_spec * filter_spec, n=padded_len, axis=0)[:TOKEN_LENGTH]
        hyena_out = (query_conv * long_conv).astype(jnp.bfloat16)
        incoming = columns_of(cotangent).astype(jnp.float32)
        conv_grad = incoming * query_conv
        query_grad = incoming * long_conv
        grad_spec = jnp.fft.rfft(conv_grad, n=padded_len, axis=0)
        gated_grad = jnp.fft.irfft(jnp.conj(filter_spec) * grad_spec, n=padded_len, axis=0)[:TOKEN_LENGTH]
        filter_grad = jnp.fft.irfft(jnp.conj(gated_spec) * grad_spec, n=padded_len, axis=0)[:TOKEN_LENGTH]
        filter_sum = filter_sum + filter_grad.reshape(TOKEN_LENGTH, width_block // FILTER_GROUPS, FILTER_GROUPS).sum(axis=1)
        grad_query = anticausal_taps(query_grad, taps_block[0]).astype(jnp.bfloat16)
        grad_key = anticausal_taps(gated_grad * value_conv, taps_block[1]).astype(jnp.bfloat16)
        grad_value = anticausal_taps(gated_grad * key_conv, taps_block[2]).astype(jnp.bfloat16)
        return filter_sum, (hyena_out, grad_query, grad_key, grad_value)

    initial = jnp.zeros((TOKEN_LENGTH, FILTER_GROUPS), jnp.float32)
    filter_total, stacked = lax.scan(one_block, initial, jnp.arange(block_count, dtype=jnp.int32))

    def unstack(blocks_out):
        return jnp.moveaxis(blocks_out, 0, 1).reshape(TOKEN_LENGTH, D)

    return (unstack(stacked[0]), unstack(stacked[1]), unstack(stacked[2]), unstack(stacked[3]), filter_total)
```

```python
import functools

import jax
import jax.numpy as jnp
import ml_dtypes
import numpy as np
from jax import lax
from jax.experimental import pallas as pl
from jax.experimental.pallas import tpu as pltpu
from jax.sharding import PartitionSpec as P

F32 = jnp.float32
BF16 = jnp.bfloat16


def halves(table):
    high = table.astype(ml_dtypes.bfloat16)
    low = (table - high.astype(np.float64)).astype(ml_dtypes.bfloat16)
    return high, low


def tables(blocks, slab, per):
    outer = 2 * blocks
    period = outer * slab
    bins = blocks + 2
    k1 = np.arange(bins)[:, None]
    used = (k1 <= blocks).astype(np.float64)
    angle = 2 * np.pi * (k1 * np.arange(blocks)[None, :] % outer) / outer
    cosine, sine = np.cos(angle), np.sin(angle)
    eye = np.eye(per)
    first = np.concatenate([np.kron(cosine * used, eye), np.kron(-sine * used, eye)], axis=0)
    weight = used * np.where((k1 == 0) | (k1 == blocks), 1.0, 2.0) / period
    last = np.kron((cosine * weight).T, eye), np.kron((-sine * weight).T, eye)
    turn = 2 * np.pi * (k1 * np.arange(slab)[None, :] % period) / period
    twist_re = np.repeat(np.cos(turn), per, axis=0).astype(np.float32)
    twist_im = np.repeat(-np.sin(turn), per, axis=0).astype(np.float32)
    spin = 2 * np.pi * (np.arange(slab)[:, None] * np.arange(slab)[None, :] % slab) / slab
    c, s = np.cos(spin), np.sin(spin)
    ahead = np.block([[c, -s], [s, c]])
    back = np.block([[c, s], [-s, c]])
    out = []
    for table in (first, ahead, back, np.concatenate(last, axis=1)):
        out.extend(halves(table))
    return out + [twist_re, twist_im]


def orders(blocks, channels):
    half = channels // 2
    i_size = half // blocks
    row = np.arange(channels)
    d, h, i = row // (2 * i_size), row // i_size % 2, row % i_size
    pick = np.zeros((channels, channels), ml_dtypes.bfloat16)
    pick[row, h * half + d * i_size + i] = 1
    fold = np.zeros((channels, half), ml_dtypes.bfloat16)
    fold[row, d * i_size + i] = 1
    return pick, fold


def dot(left, right, dims=((1,), (0,))):
    return lax.dot_general(left, right, (dims, ((), ())), preferred_element_type=F32)


def split(values):
    high = values.astype(BF16)
    return high, (values - high.astype(F32)).astype(BF16)


def unpack_kernel(in_ref, share_ref, pick_ref, fold_ref, h_ref, q_ref, k_ref, v_ref, f_ref):
    arrived = in_ref[...].astype(F32)
    share = share_ref[...].astype(F32)
    blocks, per, slab = share.shape
    pick = pick_ref[...]

    def flat(part):
        return part.reshape(blocks * per, slab).astype(BF16)

    for p, ref in enumerate((h_ref, q_ref, k_ref, v_ref)):
        ref[...] = dot(flat(arrived[:, p * per : (p + 1) * per]), pick, ((0,), (0,))).astype(BF16)
    f_ref[...] = dot(flat(share), fold_ref[...], ((0,), (0,)))


def shift(values, distance):
    slab = values.shape[2]
    lane = lax.broadcasted_iota(jnp.int32, values.shape, 2)
    turned = pltpu.roll(values, distance % slab, 2)
    edge = jnp.zeros((1,) + values.shape[1:], values.dtype)
    if distance > 0:
        return jnp.where(lane < distance, jnp.concatenate([edge, turned[:-1]], axis=0), turned)
    return jnp.where(lane >= slab + distance, jnp.concatenate([turned[1:], edge], axis=0), turned)


def taps(values, weights, sign):
    total = weights[0] * values
    for j in range(1, len(weights)):
        total = total + weights[j] * shift(values, sign * j)
    return total


RUN = 8


class Place:
    def __init__(self):
        self.seq, self.chan = lax.axis_index("seq"), lax.axis_index("chan")
        self.blocks, self.columns = lax.axis_size("seq"), lax.axis_size("chan")
        self.run = min(RUN, self.columns)
        self.work_seq, self.work_chan = self.moved(self.seq, self.chan, 2 * self.run - self.run // 2)

    def moved(self, seq, chan, distance):
        run = self.run
        z = (seq // 2 % 2 * run + chan % run + distance) % (2 * run)
        return seq // 4 * 4 + z // run * 2 + seq % 2, chan // run * run + z % run

    def worker(self, seq, chan):
        return self.moved(seq, chan, self.run // 2)

    def member(self, step):
        rows = self.blocks // 4
        row = (self.seq // 4 + step // 4 + rows // 2) % rows
        return row * 4 + (self.seq + step) % 4


def loop(count, act):
    def body(step, carry):
        act(step)
        return carry

    lax.fori_loop(0, count, body, 0)


def device(pair):
    return {"device_id": {"seq": pair[0], "chan": pair[1]}, "device_id_type": pl.DeviceIdType.MESH}


def whole_kernel(
    q_hbm, k_hbm, v_hbm, f_hbm, ct_hbm, taps_hbm, pick_hbm,
    first_hi_hbm, first_lo_hbm, ahead_hi_hbm, ahead_lo_hbm, back_hi_hbm, back_lo_hbm, last_hi_hbm, last_lo_hbm,
    twist_re_hbm, twist_im_hbm,
    out_ref, share_ref,
    q_ref, k_ref, v_ref, f_ref, ct_ref, taps_ref, pick_ref,
    first_hi, first_lo, ahead_hi, ahead_lo, back_hi, back_lo, last_hi, last_lo,
    twist_re_ref, twist_im_ref,
    packed, held, done, returned, cross_out, cross_in, total, shares,
    load_sems, send_sems, recv_sems,
):
    here = Place()
    count = here.columns
    barrier = pltpu.get_barrier_semaphore()
    blocks, rows, slab = packed.shape
    per = rows // 5
    alone = here.work_chan == here.seq

    def greet(pair):
        pl.semaphore_signal(barrier, inc=1, **device(pair))

    def towards(step):
        return (here.work_chan + 1 + step) % count

    def other(step):
        return (here.work_seq + 1 + step) % blocks

    loop(blocks, lambda step: greet((here.member(step), here.work_chan)))
    loop(blocks - 1, lambda step: greet(here.worker(other(step), here.seq)))
    pl.when(jnp.logical_not(alone))(lambda: greet(here.worker(here.work_seq, here.seq)))
    loop(count - 1, lambda step: greet(here.worker(here.work_seq, towards(step))))

    pairs = [
        (q_hbm, q_ref), (k_hbm, k_ref), (v_hbm, v_ref), (f_hbm, f_ref), (ct_hbm, ct_ref), (pick_hbm, pick_ref),
        (first_hi_hbm, first_hi), (first_lo_hbm, first_lo), (ahead_hi_hbm, ahead_hi),
        (ahead_lo_hbm, ahead_lo), (back_hi_hbm, back_hi), (back_lo_hbm, back_lo), (last_hi_hbm, last_hi),
        (last_lo_hbm, last_lo), (twist_re_hbm, twist_re_ref), (twist_im_hbm, twist_im_ref),
    ]
    loads = [pltpu.make_async_copy(source, local, load_sems.at[i]) for i, (source, local) in enumerate(pairs)]
    for load in loads:
        load.start()
    for load in loads[:6]:
        load.wait()

    high, low = split(f_ref[...])
    pick = pick_ref[...]
    parts = []
    for values in (q_ref[...], k_ref[...], v_ref[...], ct_ref[...], jnp.concatenate([high, low], axis=1)):
        parts.append(dot(pick, values, ((1,), (1,))).reshape(blocks, per, slab))
    packed[...] = jnp.concatenate(parts, axis=1).astype(BF16)

    def remote(number, source, target, pair):
        return pltpu.make_async_remote_copy(
            src_ref=source, dst_ref=target,
            send_sem=send_sems.at[number], recv_sem=recv_sems.at[number], **device(pair),
        )

    def bring(step):
        to = here.member(step)
        remote(0, packed.at[to], held.at[here.seq], here.worker(to, here.chan)).start()

    def give(step):
        to = here.member(step)
        remote(1, done.at[to], returned.at[here.work_seq], (to, here.work_chan)).start()

    def scatter(step):
        to = towards(step)
        place = here.worker(here.work_seq, to)
        remote(2, cross_out.at[to], cross_in.at[here.work_chan], place).start()

    def spread(step):
        to = (here.chan + 1 + step) % count
        remote(3, total.at[0], shares.at[here.work_seq], (here.work_chan, to)).start()

    origin = here.worker(here.seq, here.chan)
    pl.semaphore_wait(barrier, blocks + count - 1 + blocks - jnp.where(alone, 1, 0))
    taps_copy = remote(4, taps_hbm, taps_ref, origin)
    taps_copy.start()
    loop(blocks, bring)
    for load in loads[6:]:
        load.wait()
    taps_copy.wait_recv()
    channels = pick.shape[0]
    row = lax.broadcasted_iota(jnp.int32, (per, channels), 0)
    column = lax.broadcasted_iota(jnp.int32, (per, channels), 1)
    wanted = jnp.where(row < per // 2, row, row + (channels - per) // 2) + here.work_seq * (per // 2)
    choice = jnp.where(column == wanted, 1.0, 0.0).astype(F32)
    weights = []
    for p in range(3):
        own = lax.dot_general(
            choice, taps_ref[p], (((1,), (1,)), ((), ())),
            precision=lax.Precision.HIGHEST, preferred_element_type=F32,
        )
        weights.append([own[:, j : j + 1].reshape(1, per, 1) for j in range(own.shape[1])])

    remote(0, packed, held, origin).wait_recv()

    arrived = held[...].astype(F32)
    q, k, v, incoming, filt = (arrived[:, p * per : (p + 1) * per] for p in range(5))
    query_conv = taps(q, weights[0], 1)
    key_conv = taps(k, weights[1], 1)
    value_conv = taps(v, weights[2], 1)
    gated = (key_conv * value_conv).reshape(blocks * per, slab)
    conv_grad = (incoming * query_conv).reshape(blocks * per, slab)

    twist_re, twist_im = twist_re_ref[...], twist_im_ref[...]
    bins = twist_re.shape[0]

    def triple(left_hi, left_lo, right_hi, right_lo):
        return dot(left_hi, right_hi) + (dot(left_hi, right_lo) + dot(left_lo, right_hi))

    def finish(real, imag):
        turned = jnp.concatenate(
            [real * twist_re - imag * twist_im, real * twist_im + imag * twist_re], axis=1
        )
        spec = triple(*split(turned), ahead_hi[...], ahead_lo[...])
        return spec[:, :slab], spec[:, slab:]

    def inverse(real, imag):
        spec = triple(*split(jnp.concatenate([real, imag], axis=1)), back_hi[...], back_lo[...])
        real, imag = spec[:, :slab], spec[:, slab:]
        return jnp.concatenate(
            [real * twist_re + imag * twist_im, imag * twist_re - real * twist_im], axis=0
        )

    def halved(values):
        row = lax.broadcasted_iota(jnp.int32, values.shape, values.ndim - 2)
        high = values.astype(BF16).astype(F32)
        return jnp.where(row < per // 2, high, values - high).astype(BF16)

    high, low = split(jnp.concatenate([gated, conv_grad], axis=1))
    both = triple(first_hi[...], first_lo[...], high, low)
    g_re, g_im = finish(both[:bins, :slab], both[bins:, :slab])
    c_re, c_im = finish(both[:bins, slab:], both[bins:, slab:])
    cross = inverse(g_re * c_re + g_im * c_im, g_re * c_im - g_im * c_re)
    cross = triple(last_hi[...], last_lo[...], *split(cross)).reshape(blocks, per, slab)
    cross_out[...] = halved(cross + pltpu.roll(cross, per // 2, 1))

    own = (filt + pltpu.roll(filt, per // 2, 1)).reshape(blocks * per, slab)
    own = triple(first_hi[...], first_lo[...], *split(own))
    f_re, f_im = finish(own[:bins], own[bins:])
    loop(count - 1, scatter)
    kept = pltpu.make_async_copy(cross_out.at[here.work_chan], cross_in.at[here.work_chan], recv_sems.at[2])
    kept.start()
    long = inverse(g_re * f_re - g_im * f_im, g_re * f_im + g_im * f_re)
    back = inverse(f_re * c_re + f_im * c_im, f_re * c_im - f_im * c_re)
    wide = triple(last_hi[...], last_lo[...], *split(jnp.concatenate([long, back], axis=1)))
    long_conv = wide[:, :slab].reshape(blocks, per, slab)
    gated_grad = wide[:, slab:].reshape(blocks, per, slab)
    parts = [
        query_conv * long_conv,
        taps(incoming * long_conv, weights[0], -1),
        taps(gated_grad * value_conv, weights[1], -1),
        taps(gated_grad * key_conv, weights[2], -1),
    ]
    done[...] = jnp.concatenate(parts, axis=1).astype(BF16)
    loop(blocks, give)

    remote(2, cross_out, cross_in, origin).wait_recv()
    summed = jnp.sum(cross_in[...].astype(F32), axis=0, keepdims=True)
    total[...] = halved(summed + pltpu.roll(summed, per // 2, 1))
    loop(count - 1, spread)

    @pl.when(jnp.logical_not(alone))
    def _():
        spread(count - 1)
        remote(3, total.at[0], shares.at[0], origin).wait_send()

    @pl.when(alone)
    def _():
        pltpu.make_async_copy(total.at[0], shares.at[here.work_seq], recv_sems.at[3]).start()

    remote(1, done, returned, origin).wait_recv()
    out_ref[...] = returned[...]
    remote(3, shares, shares, origin).wait_recv()
    share_ref[...] = shares[...]
    taps_copy.wait_send()
    remote(0, packed, held, origin).wait_send()
    remote(1, done, returned, origin).wait_send()
    fewer = pl.ds(0, count - 1)
    remote(2, cross_out.at[fewer], cross_in.at[fewer], origin).wait_send()
    remote(3, shares.at[fewer], shares.at[fewer], origin).wait_send()


def call(body, name, outs, *operands, space=pltpu.VMEM, **more):
    return pl.pallas_call(
        body,
        name=name,
        out_shape=outs,
        in_specs=[pl.BlockSpec(memory_space=space)] * len(operands),
        out_specs=jax.tree.map(lambda _: pl.BlockSpec(memory_space=pltpu.VMEM), outs),
        **more,
    )(*operands)


def whole(query_rows, key_rows, value_rows, long_filter, cotangent, short_taps):
    slab, channels = query_rows.shape
    blocks = lax.axis_size("seq")
    per = channels // blocks
    pick, _ = orders(blocks, channels)
    shape = functools.partial(jax.ShapeDtypeStruct, dtype=BF16)
    operands = [
        query_rows, key_rows, value_rows, long_filter, cotangent, short_taps, pick,
        *tables(blocks, slab, per),
    ]
    small = pltpu.VMEM((blocks, per, slab), BF16)
    return call(
        whole_kernel,
        "whole",
        [shape((blocks, 4 * per, slab)), shape((blocks, per, slab))],
        *operands,
        space=pl.ANY,
        scratch_shapes=[
            *[pltpu.VMEM(x.shape, x.dtype) for x in operands],
            *[pltpu.VMEM((blocks, 5 * per, slab), BF16)] * 2,
            *[pltpu.VMEM((blocks, 4 * per, slab), BF16)] * 2,
            small, small, pltpu.VMEM((1, per, slab), BF16), small,
            pltpu.SemaphoreType.DMA((len(operands) - 1,)),
            *[pltpu.SemaphoreType.DMA((5,))] * 2,
        ],
        compiler_params=pltpu.CompilerParams(collective_id=0, has_side_effects=True),
    )


def unpack(returned, shares):
    blocks, per, slab = shares.shape
    channels = blocks * per
    pick, fold = orders(blocks, channels)
    outs = [jax.ShapeDtypeStruct((slab, channels), BF16)] * 4
    outs.append(jax.ShapeDtypeStruct((slab, channels // 2), F32))
    return call(unpack_kernel, "unpack", outs, returned, shares, pick, fold)


def per_device(query_rows, key_rows, value_rows, short_taps, long_filter, cotangent):
    return tuple(
        unpack(*whole(query_rows, key_rows, value_rows, long_filter, cotangent, short_taps))
    )


def solution(mesh):
    wide = P("seq", "chan")
    in_specs = (wide, wide, wide, P(None, None, "chan"), P("seq", None), wide)
    out_specs = (wide, wide, wide, wide, P("seq", None))
    return jax.shard_map(
        per_device, mesh=mesh, in_specs=in_specs, out_specs=out_specs, check_vma=False
    )
```

```python
import functools

import jax
import jax.numpy as jnp
import ml_dtypes
import numpy as np
from jax import lax
from jax.experimental import pallas as pl
from jax.experimental.pallas import tpu as pltpu
from jax.sharding import PartitionSpec as P

F32 = jnp.float32
BF16 = jnp.bfloat16


def halves(table):
    high = table.astype(ml_dtypes.bfloat16)
    low = (table - high.astype(np.float64)).astype(ml_dtypes.bfloat16)
    return high, low


def tables(blocks, slab, per):
    outer = 2 * blocks
    period = outer * slab
    bins = blocks + 2
    k1 = np.arange(bins)[:, None]
    used = (k1 <= blocks).astype(np.float64)
    angle = 2 * np.pi * (k1 * np.arange(blocks)[None, :] % outer) / outer
    cosine, sine = np.cos(angle), np.sin(angle)
    eye = np.eye(per)
    first = np.concatenate([np.kron(cosine * used, eye), np.kron(-sine * used, eye)], axis=0)
    weight = used * np.where((k1 == 0) | (k1 == blocks), 1.0, 2.0) / period
    last = np.kron((cosine * weight).T, eye), np.kron((-sine * weight).T, eye)
    turn = 2 * np.pi * (k1 * np.arange(slab)[None, :] % period) / period
    twist_re = np.repeat(np.cos(turn), per, axis=0).astype(np.float32)
    twist_im = np.repeat(-np.sin(turn), per, axis=0).astype(np.float32)
    spin = 2 * np.pi * (np.arange(slab)[:, None] * np.arange(slab)[None, :] % slab) / slab
    c, s = np.cos(spin), np.sin(spin)
    ahead = np.block([[c, -s], [s, c]])
    back = np.block([[c, s], [-s, c]])
    out = []
    for table in (first, ahead, back, np.concatenate(last, axis=1)):
        out.extend(halves(table))
    return out + [twist_re, twist_im]


def orders(blocks, channels):
    half = channels // 2
    i_size = half // blocks
    row = np.arange(channels)
    d, h, i = row // (2 * i_size), row // i_size % 2, row % i_size
    pick = np.zeros((channels, channels), ml_dtypes.bfloat16)
    pick[row, h * half + d * i_size + i] = 1
    fold = np.zeros((channels, half), ml_dtypes.bfloat16)
    fold[row, d * i_size + i] = 1
    return pick, fold


def dot(left, right, dims=((1,), (0,))):
    return lax.dot_general(left, right, (dims, ((), ())), preferred_element_type=F32)


def split(values):
    high = values.astype(BF16)
    return high, (values - high.astype(F32)).astype(BF16)


def unpack_kernel(in_ref, share_ref, pick_ref, fold_ref, h_ref, q_ref, k_ref, v_ref, f_ref):
    arrived = in_ref[...].astype(F32)
    share = share_ref[...].astype(F32)
    blocks, per, slab = share.shape
    pick = pick_ref[...]

    def flat(part):
        return part.reshape(blocks * per, slab).astype(BF16)

    for p, ref in enumerate((h_ref, q_ref, k_ref, v_ref)):
        ref[...] = dot(flat(arrived[:, p * per : (p + 1) * per]), pick, ((0,), (0,))).astype(BF16)
    f_ref[...] = dot(flat(share), fold_ref[...], ((0,), (0,)))


def shift(values, distance):
    slab = values.shape[2]
    lane = lax.broadcasted_iota(jnp.int32, values.shape, 2)
    turned = pltpu.roll(values, distance % slab, 2)
    edge = jnp.zeros((1,) + values.shape[1:], values.dtype)
    if distance > 0:
        return jnp.where(lane < distance, jnp.concatenate([edge, turned[:-1]], axis=0), turned)
    return jnp.where(lane >= slab + distance, jnp.concatenate([turned[1:], edge], axis=0), turned)


def taps(values, weights, sign):
    total = weights[0] * values
    for j in range(1, len(weights)):
        total = total + weights[j] * shift(values, sign * j)
    return total


RUN = 8


class Place:
    def __init__(self):
        self.seq, self.chan = lax.axis_index("seq"), lax.axis_index("chan")
        self.blocks, self.columns = lax.axis_size("seq"), lax.axis_size("chan")
        self.run = min(RUN, self.columns)
        self.work_seq, self.work_chan = self.moved(self.seq, self.chan, 2 * self.run - self.run // 2)

    def moved(self, seq, chan, distance):
        run = self.run
        far, column = lax.rem(lax.div(seq, 2), 2), lax.rem(chan, run)
        z = lax.rem(far * run + column + distance, 2 * run)
        there = lax.div(z, run)
        return seq + (there - far) * 2, chan - column + z - there * run

    def worker(self, seq, chan):
        return self.moved(seq, chan, self.run // 2)

    def member(self, step):
        rows = self.blocks // 4
        row = lax.rem(lax.div(self.seq, 4) + lax.div(step, 4) + rows // 2, rows)
        return row * 4 + lax.rem(self.seq + step, 4)


def loop(count, act, width=4):
    def body(turn, carry):
        for step in range(width):
            act(turn * width + step)
        return carry

    lax.fori_loop(0, count // width, body, 0)
    for step in range(count // width * width, count):
        act(jnp.int32(step))


def device(pair):
    return {"device_id": {"seq": pair[0], "chan": pair[1]}, "device_id_type": pl.DeviceIdType.MESH}


def whole_kernel(
    q_hbm, k_hbm, v_hbm, f_hbm, ct_hbm, taps_hbm, pick_hbm,
    first_hi_hbm, first_lo_hbm, ahead_hi_hbm, ahead_lo_hbm, back_hi_hbm, back_lo_hbm, last_hi_hbm, last_lo_hbm,
    twist_re_hbm, twist_im_hbm,
    out_ref, share_ref,
    q_ref, k_ref, v_ref, f_ref, ct_ref, taps_ref, pick_ref,
    first_hi, first_lo, ahead_hi, ahead_lo, back_hi, back_lo, last_hi, last_lo,
    twist_re_ref, twist_im_ref,
    packed, packed_late, held, held_late, done, done_late, returned, returned_late,
    cross_out, cross_in, total, shares,
    load_sems, send_sems, recv_sems,
):
    here = Place()
    count = here.columns
    barrier = pltpu.get_barrier_semaphore()
    blocks, rows, slab = packed.shape
    per = rows // 4
    alone = here.work_chan == here.seq

    def greet(pair):
        pl.semaphore_signal(barrier, inc=1, **device(pair))

    def towards(step):
        return lax.rem(here.work_chan + 1 + step, count)

    def other(step):
        return lax.rem(here.work_seq + 1 + step, blocks)

    loop(blocks - 1, lambda step: greet(here.worker(other(step), here.seq)))
    pl.when(jnp.logical_not(alone))(lambda: greet(here.worker(here.work_seq, here.seq)))
    loop(count - 1, lambda step: greet(here.worker(here.work_seq, towards(step))))
    loop(blocks, lambda step: greet((here.member(step), here.work_chan)))

    pairs = [
        (q_hbm, q_ref), (k_hbm, k_ref), (v_hbm, v_ref), (f_hbm, f_ref), (ct_hbm, ct_ref), (pick_hbm, pick_ref),
        (first_hi_hbm, first_hi), (first_lo_hbm, first_lo), (ahead_hi_hbm, ahead_hi),
        (ahead_lo_hbm, ahead_lo), (back_hi_hbm, back_hi), (back_lo_hbm, back_lo), (last_hi_hbm, last_hi),
        (last_lo_hbm, last_lo), (twist_re_hbm, twist_re_ref), (twist_im_hbm, twist_im_ref),
    ]
    loads = [pltpu.make_async_copy(source, local, load_sems.at[i]) for i, (source, local) in enumerate(pairs)]
    for load in loads:
        load.start()
    for load in loads[:6]:
        load.wait()

    high, low = split(f_ref[...])
    pick = pick_ref[...]

    def pack(*parts):
        parts = [dot(pick, values, ((1,), (1,))).reshape(blocks, per, slab) for values in parts]
        return jnp.concatenate(parts, axis=1).astype(BF16)

    packed[...] = pack(k_ref[...], v_ref[...], q_ref[...], ct_ref[...])
    packed_late[...] = pack(jnp.concatenate([high, low], axis=1))

    def remote(number, source, target, pair):
        return pltpu.make_async_remote_copy(
            src_ref=source, dst_ref=target,
            send_sem=send_sems.at[number], recv_sem=recv_sems.at[number], **device(pair),
        )

    def bring(step):
        to = here.member(step)
        remote(0, packed.at[to], held.at[here.seq], here.worker(to, here.chan)).start()

    def bring_late(step):
        to = here.member(step)
        remote(5, packed_late.at[to], held_late.at[here.seq], here.worker(to, here.chan)).start()

    def give(step):
        to = here.member(step)
        remote(1, done.at[to], returned.at[here.work_seq], (to, here.work_chan)).start()

    def give_late(step):
        to = here.member(step)
        remote(6, done_late.at[to], returned_late.at[here.work_seq], (to, here.work_chan)).start()

    def scatter(step):
        to = towards(step)
        place = here.worker(here.work_seq, to)
        remote(2, cross_out.at[to], cross_in.at[here.work_chan], place).start()

    def spread(step):
        to = lax.rem(here.chan + 1 + step, count)
        remote(3, total.at[0], shares.at[here.work_seq], (here.work_chan, to)).start()

    origin = here.worker(here.seq, here.chan)
    pl.semaphore_wait(barrier, blocks + count - 1 + blocks - jnp.where(alone, 1, 0))
    taps_copy = remote(4, taps_hbm, taps_ref, origin)
    taps_copy.start()
    loop(blocks, bring)
    loop(blocks, bring_late)
    for load in loads[6:]:
        load.wait()
    taps_copy.wait_recv()
    channels = pick.shape[0]
    row = lax.broadcasted_iota(jnp.int32, (per, channels), 0)
    column = lax.broadcasted_iota(jnp.int32, (per, channels), 1)
    wanted = jnp.where(row < per // 2, row, row + (channels - per) // 2) + here.work_seq * (per // 2)
    choice = jnp.where(column == wanted, 1.0, 0.0).astype(F32)
    weights = []
    for p in range(3):
        own = lax.dot_general(
            choice, taps_ref[p], (((1,), (1,)), ((), ())),
            precision=lax.Precision.HIGHEST, preferred_element_type=F32,
        )
        weights.append([own[:, j : j + 1].reshape(1, per, 1) for j in range(own.shape[1])])

    remote(0, packed, held, origin).wait_recv()

    arrived = held[...].astype(F32)
    k, v, q, incoming = (arrived[:, p * per : (p + 1) * per] for p in range(4))
    key_conv = taps(k, weights[1], 1)
    value_conv = taps(v, weights[2], 1)
    gated = (key_conv * value_conv).reshape(blocks * per, slab)
    query_conv = taps(q, weights[0], 1)
    conv_grad = (incoming * query_conv).reshape(blocks * per, slab)

    twist_re, twist_im = twist_re_ref[...], twist_im_ref[...]
    bins = twist_re.shape[0]

    def triple(left_hi, left_lo, right_hi, right_lo):
        return dot(left_hi, right_hi) + (dot(left_hi, right_lo) + dot(left_lo, right_hi))

    def finish(real, imag):
        turned = jnp.concatenate(
            [real * twist_re - imag * twist_im, real * twist_im + imag * twist_re], axis=1
        )
        spec = triple(*split(turned), ahead_hi[...], ahead_lo[...])
        return spec[:, :slab], spec[:, slab:]

    def inverse(real, imag):
        spec = triple(*split(jnp.concatenate([real, imag], axis=1)), back_hi[...], back_lo[...])
        real, imag = spec[:, :slab], spec[:, slab:]
        return jnp.concatenate(
            [real * twist_re + imag * twist_im, imag * twist_re - real * twist_im], axis=0
        )

    def halved(values):
        row = lax.broadcasted_iota(jnp.int32, values.shape, values.ndim - 2)
        high = values.astype(BF16).astype(F32)
        return jnp.where(row < per // 2, high, values - high).astype(BF16)

    def ahead(values):
        both = triple(first_hi[...], first_lo[...], *split(values))
        return [
            finish(both[:bins, at : at + slab], both[bins:, at : at + slab])
            for at in range(0, values.shape[1], slab)
        ]

    def behind(values):
        return triple(last_hi[...], last_lo[...], *split(values)).reshape(blocks, per, slab)

    (g_re, g_im), (c_re, c_im) = ahead(jnp.concatenate([gated, conv_grad], axis=1))
    cross = behind(inverse(g_re * c_re + g_im * c_im, g_re * c_im - g_im * c_re))
    cross_out[...] = halved(cross + pltpu.roll(cross, per // 2, 1))
    loop(count - 1, scatter)
    kept = pltpu.make_async_copy(cross_out.at[here.work_chan], cross_in.at[here.work_chan], recv_sems.at[2])
    kept.start()

    remote(5, packed_late, held_late, origin).wait_recv()
    filt = held_late[...].astype(F32)
    filt = (filt + pltpu.roll(filt, per // 2, 1)).reshape(blocks * per, slab)
    ((f_re, f_im),) = ahead(filt)
    long_conv = behind(inverse(g_re * f_re - g_im * f_im, g_re * f_im + g_im * f_re))
    parts = [query_conv * long_conv, taps(incoming * long_conv, weights[0], -1)]
    done[...] = jnp.concatenate(parts, axis=1).astype(BF16)
    loop(blocks, give)
    gated_grad = behind(inverse(f_re * c_re + f_im * c_im, f_re * c_im - f_im * c_re))
    parts = [
        taps(gated_grad * value_conv, weights[1], -1),
        taps(gated_grad * key_conv, weights[2], -1),
    ]
    done_late[...] = jnp.concatenate(parts, axis=1).astype(BF16)

    remote(2, cross_out, cross_in, origin).wait_recv()
    summed = jnp.sum(cross_in[...].astype(F32), axis=0, keepdims=True)
    total[...] = halved(summed + pltpu.roll(summed, per // 2, 1))
    loop(count - 1, spread)

    @pl.when(jnp.logical_not(alone))
    def _():
        spread(jnp.int32(count - 1))

    @pl.when(alone)
    def _():
        pltpu.make_async_copy(total.at[0], shares.at[here.work_seq], recv_sems.at[3]).start()

    loop(blocks, give_late)
    remote(1, done, returned, origin).wait_recv()
    out_ref[:, : 2 * per] = returned[...]
    remote(6, done_late, returned_late, origin).wait_recv()
    out_ref[:, 2 * per :] = returned_late[...]
    remote(3, shares, shares, origin).wait_recv()
    share_ref[...] = shares[...]
    taps_copy.wait_send()
    remote(0, packed, held, origin).wait_send()
    remote(1, done, returned, origin).wait_send()
    remote(5, packed_late, held_late, origin).wait_send()
    remote(6, done_late, returned_late, origin).wait_send()
    fewer = pl.ds(0, count - 1)
    remote(2, cross_out.at[fewer], cross_in.at[fewer], origin).wait_send()
    remote(3, shares.at[fewer], shares.at[fewer], origin).wait_send()
    pl.when(jnp.logical_not(alone))(lambda: remote(3, total.at[0], shares.at[0], origin).wait_send())


def call(body, name, outs, *operands, space=pltpu.VMEM, **more):
    return pl.pallas_call(
        body,
        name=name,
        out_shape=outs,
        in_specs=[pl.BlockSpec(memory_space=space)] * len(operands),
        out_specs=jax.tree.map(lambda _: pl.BlockSpec(memory_space=pltpu.VMEM), outs),
        **more,
    )(*operands)


def whole(query_rows, key_rows, value_rows, long_filter, cotangent, short_taps):
    slab, channels = query_rows.shape
    blocks = lax.axis_size("seq")
    per = channels // blocks
    pick, _ = orders(blocks, channels)
    shape = functools.partial(jax.ShapeDtypeStruct, dtype=BF16)
    operands = [
        query_rows, key_rows, value_rows, long_filter, cotangent, short_taps, pick,
        *tables(blocks, slab, per),
    ]
    small = pltpu.VMEM((blocks, per, slab), BF16)
    return call(
        whole_kernel,
        "whole",
        [shape((blocks, 4 * per, slab)), shape((blocks, per, slab))],
        *operands,
        space=pl.ANY,
        scratch_shapes=[
            *[pltpu.VMEM(x.shape, x.dtype) for x in operands],
            *[pltpu.VMEM((blocks, n * per, slab), BF16) for n in (4, 1, 4, 1, 2, 2, 2, 2)],
            small, small, pltpu.VMEM((1, per, slab), BF16), small,
            pltpu.SemaphoreType.DMA((len(operands) - 1,)),
            *[pltpu.SemaphoreType.DMA((7,))] * 2,
        ],
        compiler_params=pltpu.CompilerParams(collective_id=0, has_side_effects=True),
    )


def unpack(returned, shares):
    blocks, per, slab = shares.shape
    channels = blocks * per
    pick, fold = orders(blocks, channels)
    outs = [jax.ShapeDtypeStruct((slab, channels), BF16)] * 4
    outs.append(jax.ShapeDtypeStruct((slab, channels // 2), F32))
    return call(unpack_kernel, "unpack", outs, returned, shares, pick, fold)


def per_device(query_rows, key_rows, value_rows, short_taps, long_filter, cotangent):
    return tuple(
        unpack(*whole(query_rows, key_rows, value_rows, long_filter, cotangent, short_taps))
    )


def solution(mesh):
    wide = P("seq", "chan")
    in_specs = (wide, wide, wide, P(None, None, "chan"), P("seq", None), wide)
    out_specs = (wide, wide, wide, wide, P("seq", None))
    return jax.shard_map(
        per_device, mesh=mesh, in_specs=in_specs, out_specs=out_specs, check_vma=False
    )
```

```python
import functools

import jax
import jax.numpy as jnp
import ml_dtypes
import numpy as np
from jax import lax
from jax.experimental import pallas as pl
from jax.experimental.pallas import tpu as pltpu
from jax.sharding import PartitionSpec as P

F32 = jnp.float32
BF16 = jnp.bfloat16


def halves(table):
    high = table.astype(ml_dtypes.bfloat16)
    low = (table - high.astype(np.float64)).astype(ml_dtypes.bfloat16)
    return high, low


def tables(blocks, slab, per):
    outer = 2 * blocks
    period = outer * slab
    bins = blocks + 2
    k1 = np.arange(bins)[:, None]
    used = (k1 <= blocks).astype(np.float64)
    angle = 2 * np.pi * (k1 * np.arange(blocks)[None, :] % outer) / outer
    cosine, sine = np.cos(angle), np.sin(angle)
    eye = np.eye(per)
    first = np.concatenate([np.kron(cosine * used, eye), np.kron(-sine * used, eye)], axis=0)
    weight = used * np.where((k1 == 0) | (k1 == blocks), 1.0, 2.0) / period
    last = np.kron((cosine * weight).T, eye), np.kron((-sine * weight).T, eye)
    turn = 2 * np.pi * (k1 * np.arange(slab)[None, :] % period) / period
    twist_re = np.repeat(np.cos(turn), per, axis=0).astype(np.float32)
    twist_im = np.repeat(-np.sin(turn), per, axis=0).astype(np.float32)
    spin = 2 * np.pi * (np.arange(slab)[:, None] * np.arange(slab)[None, :] % slab) / slab
    c, s = np.cos(spin), np.sin(spin)
    ahead = np.block([[c, -s], [s, c]])
    back = np.block([[c, s], [-s, c]])
    out = []
    for table in (first, ahead, back, np.concatenate(last, axis=1)):
        out.extend(halves(table))
    return out + [twist_re, twist_im]


def orders(blocks, channels):
    half = channels // 2
    i_size = half // blocks
    row = np.arange(channels)
    d, h, i = row // (2 * i_size), row // i_size % 2, row % i_size
    pick = np.zeros((channels, channels), ml_dtypes.bfloat16)
    pick[row, h * half + d * i_size + i] = 1
    fold = np.zeros((channels, half), ml_dtypes.bfloat16)
    fold[row, d * i_size + i] = 1
    return pick, fold


def dot(left, right, dims=((1,), (0,))):
    return lax.dot_general(left, right, (dims, ((), ())), preferred_element_type=F32)


def split(values):
    high = values.astype(BF16)
    return high, (values - high.astype(F32)).astype(BF16)


def unpack_kernel(in_ref, share_ref, pick_ref, fold_ref, h_ref, q_ref, k_ref, v_ref, f_ref):
    arrived = in_ref[...].astype(F32)
    share = share_ref[...].astype(F32)
    blocks, per, slab = share.shape
    pick = pick_ref[...]

    def flat(part):
        return part.reshape(blocks * per, slab).astype(BF16)

    for p, ref in enumerate((h_ref, q_ref, k_ref, v_ref)):
        ref[...] = dot(flat(arrived[:, p * per : (p + 1) * per]), pick, ((0,), (0,))).astype(BF16)
    f_ref[...] = dot(flat(share), fold_ref[...], ((0,), (0,)))


def shift(values, distance):
    slab = values.shape[2]
    lane = lax.broadcasted_iota(jnp.int32, values.shape, 2)
    turned = pltpu.roll(values, distance % slab, 2)
    edge = jnp.zeros((1,) + values.shape[1:], values.dtype)
    if distance > 0:
        return jnp.where(lane < distance, jnp.concatenate([edge, turned[:-1]], axis=0), turned)
    return jnp.where(lane >= slab + distance, jnp.concatenate([turned[1:], edge], axis=0), turned)


def taps(values, weights, sign):
    total = weights[0] * values
    for j in range(1, len(weights)):
        total = total + weights[j] * shift(values, sign * j)
    return total


RUN = 8


class Place:
    def __init__(self):
        self.seq, self.chan = lax.axis_index("seq"), lax.axis_index("chan")
        self.blocks, self.columns = lax.axis_size("seq"), lax.axis_size("chan")
        self.run = min(RUN, self.columns)
        self.work_seq, self.work_chan = self.moved(self.seq, self.chan, 2 * self.run - self.run // 2)

    def moved(self, seq, chan, distance):
        run = self.run
        far, column = lax.rem(lax.div(seq, 2), 2), lax.rem(chan, run)
        z = lax.rem(far * run + column + distance, 2 * run)
        there = lax.div(z, run)
        return seq + (there - far) * 2, chan - column + z - there * run

    def worker(self, seq, chan):
        return self.moved(seq, chan, self.run // 2)

    def member(self, step):
        rows = self.blocks // 4
        row = lax.rem(lax.div(self.seq, 4) + lax.div(step, 4) + rows // 2, rows)
        return row * 4 + lax.rem(self.seq + step, 4)


def loop(count, act, width=4):
    def body(turn, carry):
        for step in range(width):
            act(turn * width + step)
        return carry

    lax.fori_loop(0, count // width, body, 0)
    for step in range(count // width * width, count):
        act(jnp.int32(step))


def device(pair):
    return {"device_id": {"seq": pair[0], "chan": pair[1]}, "device_id_type": pl.DeviceIdType.MESH}


def whole_kernel(
    q_hbm, k_hbm, v_hbm, f_hbm, ct_hbm, taps_hbm, pick_hbm,
    first_hi_hbm, first_lo_hbm, ahead_hi_hbm, ahead_lo_hbm, back_hi_hbm, back_lo_hbm, last_hi_hbm, last_lo_hbm,
    twist_re_hbm, twist_im_hbm,
    out_ref, share_ref,
    q_ref, k_ref, v_ref, f_ref, ct_ref, taps_ref, pick_ref,
    first_hi, first_lo, ahead_hi, ahead_lo, back_hi, back_lo, last_hi, last_lo,
    twist_re_ref, twist_im_ref,
    packed, packed_late, held, held_late, done, done_late, returned, returned_late,
    cross_out, cross_in, total, shares,
    load_sems, send_sems, recv_sems,
):
    here = Place()
    count = here.columns
    barrier = pltpu.get_barrier_semaphore()
    blocks, rows, slab = packed.shape
    per = rows // 3
    alone = here.work_chan == here.seq

    def greet(pair):
        pl.semaphore_signal(barrier, inc=1, **device(pair))

    def towards(step):
        return lax.rem(here.work_chan + 1 + step, count)

    loop(count - 1, lambda step: greet(here.worker(here.work_seq, towards(step))))
    loop(blocks, lambda step: greet((here.member(step), here.work_chan)))

    pairs = [
        (q_hbm, q_ref), (k_hbm, k_ref), (v_hbm, v_ref), (f_hbm, f_ref), (ct_hbm, ct_ref), (pick_hbm, pick_ref),
        (first_hi_hbm, first_hi), (first_lo_hbm, first_lo), (ahead_hi_hbm, ahead_hi),
        (ahead_lo_hbm, ahead_lo), (back_hi_hbm, back_hi), (back_lo_hbm, back_lo), (last_hi_hbm, last_hi),
        (last_lo_hbm, last_lo), (twist_re_hbm, twist_re_ref), (twist_im_hbm, twist_im_ref),
    ]
    loads = [pltpu.make_async_copy(source, local, load_sems.at[i]) for i, (source, local) in enumerate(pairs)]
    for load in loads:
        load.start()
    for load in loads[:6]:
        load.wait()

    high, low = split(f_ref[...])
    pick = pick_ref[...]

    def pack(*parts):
        parts = [dot(pick, values, ((1,), (1,))).reshape(blocks, per, slab) for values in parts]
        return jnp.concatenate(parts, axis=1).astype(BF16)

    packed[...] = pack(k_ref[...], v_ref[...], jnp.concatenate([high, low], axis=1))
    packed_late[...] = pack(q_ref[...], ct_ref[...])

    def remote(number, source, target, pair):
        return pltpu.make_async_remote_copy(
            src_ref=source, dst_ref=target,
            send_sem=send_sems.at[number], recv_sem=recv_sems.at[number], **device(pair),
        )

    def bring(step):
        to = here.member(step)
        remote(0, packed.at[to], held.at[here.seq], here.worker(to, here.chan)).start()

    def bring_late(step):
        to = here.member(step)
        remote(5, packed_late.at[to], held_late.at[here.seq], here.worker(to, here.chan)).start()

    def give(step):
        to = here.member(step)
        remote(1, done.at[to], returned.at[here.work_seq], (to, here.work_chan)).start()

    def give_late(step):
        to = here.member(step)
        remote(6, done_late.at[to], returned_late.at[here.work_seq], (to, here.work_chan)).start()

    def scatter(step):
        to = towards(step)
        place = here.worker(here.work_seq, to)
        remote(2, cross_out.at[to], cross_in.at[here.work_chan], place).start()

    def spread(step):
        to = lax.rem(here.chan + 1 + step, count)
        remote(3, total.at[0], shares.at[here.work_seq], (here.work_chan, to)).start()

    origin = here.worker(here.seq, here.chan)
    pl.semaphore_wait(barrier, blocks + count - 1)
    taps_copy = remote(4, taps_hbm, taps_ref, origin)
    taps_copy.start()
    loop(blocks, bring)
    loop(blocks, bring_late)
    for load in loads[6:]:
        load.wait()
    taps_copy.wait_recv()
    channels = pick.shape[0]
    row = lax.broadcasted_iota(jnp.int32, (per, channels), 0)
    column = lax.broadcasted_iota(jnp.int32, (per, channels), 1)
    wanted = jnp.where(row < per // 2, row, row + (channels - per) // 2) + here.work_seq * (per // 2)
    choice = jnp.where(column == wanted, 1.0, 0.0).astype(F32)
    weights = []
    for p in range(3):
        own = lax.dot_general(
            choice, taps_ref[p], (((1,), (1,)), ((), ())),
            precision=lax.Precision.HIGHEST, preferred_element_type=F32,
        )
        weights.append([own[:, j : j + 1].reshape(1, per, 1) for j in range(own.shape[1])])

    remote(0, packed, held, origin).wait_recv()

    arrived = held[...].astype(F32)
    k, v, filt = (arrived[:, p * per : (p + 1) * per] for p in range(3))
    key_conv = taps(k, weights[1], 1)
    value_conv = taps(v, weights[2], 1)
    gated = (key_conv * value_conv).reshape(blocks * per, slab)
    filt = (filt + pltpu.roll(filt, per // 2, 1)).reshape(blocks * per, slab)

    twist_re, twist_im = twist_re_ref[...], twist_im_ref[...]
    bins = twist_re.shape[0]

    def triple(left_hi, left_lo, right_hi, right_lo):
        return dot(left_hi, right_hi) + (dot(left_hi, right_lo) + dot(left_lo, right_hi))

    def finish(real, imag):
        turned = jnp.concatenate(
            [real * twist_re - imag * twist_im, real * twist_im + imag * twist_re], axis=1
        )
        spec = triple(*split(turned), ahead_hi[...], ahead_lo[...])
        return spec[:, :slab], spec[:, slab:]

    def inverse(real, imag):
        spec = triple(*split(jnp.concatenate([real, imag], axis=1)), back_hi[...], back_lo[...])
        real, imag = spec[:, :slab], spec[:, slab:]
        return jnp.concatenate(
            [real * twist_re + imag * twist_im, imag * twist_re - real * twist_im], axis=0
        )

    def halved(values):
        row = lax.broadcasted_iota(jnp.int32, values.shape, values.ndim - 2)
        high = values.astype(BF16).astype(F32)
        return jnp.where(row < per // 2, high, values - high).astype(BF16)

    def ahead(values):
        both = triple(first_hi[...], first_lo[...], *split(values))
        return [
            finish(both[:bins, at : at + slab], both[bins:, at : at + slab])
            for at in range(0, values.shape[1], slab)
        ]

    def behind(values):
        return triple(last_hi[...], last_lo[...], *split(values)).reshape(blocks, per, slab)

    (g_re, g_im), (f_re, f_im) = ahead(jnp.concatenate([gated, filt], axis=1))
    long_conv = behind(inverse(g_re * f_re - g_im * f_im, g_re * f_im + g_im * f_re))

    remote(5, packed_late, held_late, origin).wait_recv()
    arrived = held_late[...].astype(F32)
    q, incoming = arrived[:, :per], arrived[:, per:]
    query_conv = taps(q, weights[0], 1)
    ((c_re, c_im),) = ahead((incoming * query_conv).reshape(blocks * per, slab))
    cross = behind(inverse(g_re * c_re + g_im * c_im, g_re * c_im - g_im * c_re))
    cross_out[...] = halved(cross + pltpu.roll(cross, per // 2, 1))
    parts = [query_conv * long_conv, taps(incoming * long_conv, weights[0], -1)]
    done[...] = jnp.concatenate(parts, axis=1).astype(BF16)
    loop(count - 1, scatter)
    kept = pltpu.make_async_copy(cross_out.at[here.work_chan], cross_in.at[here.work_chan], recv_sems.at[2])
    kept.start()
    loop(blocks, give)
    gated_grad = behind(inverse(f_re * c_re + f_im * c_im, f_re * c_im - f_im * c_re))
    parts = [
        taps(gated_grad * value_conv, weights[1], -1),
        taps(gated_grad * key_conv, weights[2], -1),
    ]
    done_late[...] = jnp.concatenate(parts, axis=1).astype(BF16)
    loop(blocks, give_late)

    remote(2, cross_out, cross_in, origin).wait_recv()
    summed = jnp.sum(cross_in[...].astype(F32), axis=0, keepdims=True)
    total[...] = halved(summed + pltpu.roll(summed, per // 2, 1))
    loop(count - 1, spread)

    @pl.when(jnp.logical_not(alone))
    def _():
        spread(jnp.int32(count - 1))
        remote(3, total.at[0], shares.at[0], origin).wait_send()

    @pl.when(alone)
    def _():
        pltpu.make_async_copy(total.at[0], shares.at[here.work_seq], recv_sems.at[3]).start()

    remote(1, done, returned, origin).wait_recv()
    out_ref[:, : 2 * per] = returned[...]
    remote(6, done_late, returned_late, origin).wait_recv()
    out_ref[:, 2 * per :] = returned_late[...]
    remote(3, shares, shares, origin).wait_recv()
    share_ref[...] = shares[...]
    taps_copy.wait_send()
    remote(0, packed, held, origin).wait_send()
    remote(1, done, returned, origin).wait_send()
    remote(5, packed_late, held_late, origin).wait_send()
    remote(6, done_late, returned_late, origin).wait_send()
    fewer = pl.ds(0, count - 1)
    remote(2, cross_out.at[fewer], cross_in.at[fewer], origin).wait_send()
    remote(3, shares.at[fewer], shares.at[fewer], origin).wait_send()


def call(body, name, outs, *operands, space=pltpu.VMEM, **more):
    return pl.pallas_call(
        body,
        name=name,
        out_shape=outs,
        in_specs=[pl.BlockSpec(memory_space=space)] * len(operands),
        out_specs=jax.tree.map(lambda _: pl.BlockSpec(memory_space=pltpu.VMEM), outs),
        **more,
    )(*operands)


def whole(query_rows, key_rows, value_rows, long_filter, cotangent, short_taps):
    slab, channels = query_rows.shape
    blocks = lax.axis_size("seq")
    per = channels // blocks
    pick, _ = orders(blocks, channels)
    shape = functools.partial(jax.ShapeDtypeStruct, dtype=BF16)
    operands = [
        query_rows, key_rows, value_rows, long_filter, cotangent, short_taps, pick,
        *tables(blocks, slab, per),
    ]
    small = pltpu.VMEM((blocks, per, slab), BF16)
    return call(
        whole_kernel,
        "whole",
        [shape((blocks, 4 * per, slab)), shape((blocks, per, slab))],
        *operands,
        space=pl.ANY,
        scratch_shapes=[
            *[pltpu.VMEM(x.shape, x.dtype) for x in operands],
            *[pltpu.VMEM((blocks, n * per, slab), BF16) for n in (3, 2, 3, 2, 2, 2, 2, 2)],
            small, small, pltpu.VMEM((1, per, slab), BF16), small,
            pltpu.SemaphoreType.DMA((len(operands) - 1,)),
            *[pltpu.SemaphoreType.DMA((7,))] * 2,
        ],
        compiler_params=pltpu.CompilerParams(collective_id=0, has_side_effects=True),
    )


def unpack(returned, shares):
    blocks, per, slab = shares.shape
    channels = blocks * per
    pick, fold = orders(blocks, channels)
    outs = [jax.ShapeDtypeStruct((slab, channels), BF16)] * 4
    outs.append(jax.ShapeDtypeStruct((slab, channels // 2), F32))
    return call(unpack_kernel, "unpack", outs, returned, shares, pick, fold)


def per_device(query_rows, key_rows, value_rows, short_taps, long_filter, cotangent):
    return tuple(
        unpack(*whole(query_rows, key_rows, value_rows, long_filter, cotangent, short_taps))
    )


def solution(mesh):
    wide = P("seq", "chan")
    in_specs = (wide, wide, wide, P(None, None, "chan"), P("seq", None), wide)
    out_specs = (wide, wide, wide, wide, P("seq", None))
    return jax.shard_map(
        per_device, mesh=mesh, in_specs=in_specs, out_specs=out_specs, check_vma=False
    )
```

```python
import functools

import jax
import jax.numpy as jnp
import ml_dtypes
import numpy as np
from jax import lax
from jax.experimental import pallas as pl
from jax.experimental.pallas import tpu as pltpu
from jax.sharding import PartitionSpec as P

F32 = jnp.float32
BF16 = jnp.bfloat16


def halves(table):
    high = table.astype(ml_dtypes.bfloat16)
    low = (table - high.astype(np.float64)).astype(ml_dtypes.bfloat16)
    return high, low


def tables(blocks, slab, per):
    outer = 2 * blocks
    period = outer * slab
    bins = blocks + 2
    k1 = np.arange(bins)[:, None]
    used = (k1 <= blocks).astype(np.float64)
    angle = 2 * np.pi * (k1 * np.arange(blocks)[None, :] % outer) / outer
    cosine, sine = np.cos(angle), np.sin(angle)
    eye = np.eye(per)
    first = np.concatenate([np.kron(cosine * used, eye), np.kron(-sine * used, eye)], axis=0)
    weight = used * np.where((k1 == 0) | (k1 == blocks), 1.0, 2.0) / period
    last = np.kron((cosine * weight).T, eye), np.kron((-sine * weight).T, eye)
    turn = 2 * np.pi * (k1 * np.arange(slab)[None, :] % period) / period
    twist_re = np.repeat(np.cos(turn), per, axis=0).astype(np.float32)
    twist_im = np.repeat(-np.sin(turn), per, axis=0).astype(np.float32)
    spin = 2 * np.pi * (np.arange(slab)[:, None] * np.arange(slab)[None, :] % slab) / slab
    c, s = np.cos(spin), np.sin(spin)
    ahead = np.block([[c, -s], [s, c]])
    back = np.block([[c, s], [-s, c]])
    out = []
    for table in (first, ahead, back, np.concatenate(last, axis=1)):
        out.extend(halves(table))
    return out + [twist_re, twist_im]


def orders(blocks, channels):
    half = channels // 2
    i_size = half // blocks
    row = np.arange(channels)
    d, h, i = row // (2 * i_size), row // i_size % 2, row % i_size
    pick = np.zeros((channels, channels), ml_dtypes.bfloat16)
    pick[row, h * half + d * i_size + i] = 1
    fold = np.zeros((channels, half), ml_dtypes.bfloat16)
    fold[row, d * i_size + i] = 1
    return pick, fold


def dot(left, right, dims=((1,), (0,))):
    return lax.dot_general(left, right, (dims, ((), ())), preferred_element_type=F32)


def split(values):
    high = values.astype(BF16)
    return high, (values - high.astype(F32)).astype(BF16)


def unpack_kernel(in_ref, share_ref, pick_ref, fold_ref, h_ref, q_ref, k_ref, v_ref, f_ref):
    arrived = in_ref[...].astype(F32)
    share = share_ref[...].astype(F32)
    blocks, per, slab = share.shape
    pick = pick_ref[...]

    def flat(part):
        return part.reshape(blocks * per, slab).astype(BF16)

    for p, ref in enumerate((h_ref, q_ref, k_ref, v_ref)):
        ref[...] = dot(flat(arrived[:, p * per : (p + 1) * per]), pick, ((0,), (0,))).astype(BF16)
    f_ref[...] = dot(flat(share), fold_ref[...], ((0,), (0,)))


def shift(values, distance):
    slab = values.shape[2]
    lane = lax.broadcasted_iota(jnp.int32, values.shape, 2)
    turned = pltpu.roll(values, distance % slab, 2)
    edge = jnp.zeros((1,) + values.shape[1:], values.dtype)
    if distance > 0:
        return jnp.where(lane < distance, jnp.concatenate([edge, turned[:-1]], axis=0), turned)
    return jnp.where(lane >= slab + distance, jnp.concatenate([turned[1:], edge], axis=0), turned)


def taps(values, weights, sign):
    total = weights[0] * values
    for j in range(1, len(weights)):
        total = total + weights[j] * shift(values, sign * j)
    return total


RUN = 8


class Place:
    def __init__(self):
        self.seq, self.chan = lax.axis_index("seq"), lax.axis_index("chan")
        self.blocks, self.columns = lax.axis_size("seq"), lax.axis_size("chan")
        self.run = min(RUN, self.columns)
        self.work_seq, self.work_chan = self.moved(self.seq, self.chan, 2 * self.run - self.run // 2)

    def moved(self, seq, chan, distance):
        run = self.run
        far, column = lax.rem(lax.div(seq, 2), 2), lax.rem(chan, run)
        z = lax.rem(far * run + column + distance, 2 * run)
        there = lax.div(z, run)
        return seq + (there - far) * 2, chan - column + z - there * run

    def worker(self, seq, chan):
        return self.moved(seq, chan, self.run // 2)

    def block(self, chan):
        half = self.run // 2
        column = lax.rem(chan, self.run)
        far = lax.rem(lax.rem(lax.div(self.work_seq, 2), 2) + lax.div(column, half), 2)
        order = lax.div(chan, self.run) * half + lax.rem(column, half)
        return lax.div(order, 2) * 4 + far * 2 + lax.rem(order, 2)

    def member(self, step):
        rows = self.blocks // 4
        row = lax.rem(lax.div(self.seq, 4) + lax.div(step, 4) + rows // 2, rows)
        return row * 4 + lax.rem(self.seq + step, 4)


def loop(count, act, width=4):
    def body(turn, carry):
        for step in range(width):
            act(turn * width + step)
        return carry

    lax.fori_loop(0, count // width, body, 0)
    for step in range(count // width * width, count):
        act(jnp.int32(step))


def device(pair):
    return {"device_id": {"seq": pair[0], "chan": pair[1]}, "device_id_type": pl.DeviceIdType.MESH}


def whole_kernel(
    q_hbm, k_hbm, v_hbm, f_hbm, ct_hbm, taps_hbm, pick_hbm,
    first_hi_hbm, first_lo_hbm, ahead_hi_hbm, ahead_lo_hbm, back_hi_hbm, back_lo_hbm, last_hi_hbm, last_lo_hbm,
    twist_re_hbm, twist_im_hbm,
    out_ref, share_ref,
    q_ref, k_ref, v_ref, f_ref, ct_ref, taps_ref, pick_ref,
    first_hi, first_lo, ahead_hi, ahead_lo, back_hi, back_lo, last_hi, last_lo,
    twist_re_ref, twist_im_ref,
    packed, packed_late, held, held_late, done, done_late, returned, returned_late,
    cross_out, cross_in, total, shares,
    load_sems, send_sems, recv_sems,
):
    here = Place()
    count = here.columns
    barrier = pltpu.get_barrier_semaphore()
    blocks, rows, slab = packed.shape
    per = rows // 3
    target = here.block(here.work_chan)
    alone = target == here.seq

    def greet(pair):
        pl.semaphore_signal(barrier, inc=1, **device(pair))

    def towards(step):
        return lax.rem(here.work_chan + 1 + step, count)

    loop(count - 1, lambda step: greet(here.worker(here.work_seq, towards(step))))
    loop(blocks, lambda step: greet((here.member(step), here.work_chan)))

    pairs = [
        (q_hbm, q_ref), (k_hbm, k_ref), (v_hbm, v_ref), (f_hbm, f_ref), (ct_hbm, ct_ref), (pick_hbm, pick_ref),
        (first_hi_hbm, first_hi), (first_lo_hbm, first_lo), (ahead_hi_hbm, ahead_hi),
        (ahead_lo_hbm, ahead_lo), (back_hi_hbm, back_hi), (back_lo_hbm, back_lo), (last_hi_hbm, last_hi),
        (last_lo_hbm, last_lo), (twist_re_hbm, twist_re_ref), (twist_im_hbm, twist_im_ref),
    ]
    loads = [pltpu.make_async_copy(source, local, load_sems.at[i]) for i, (source, local) in enumerate(pairs)]
    for load in loads:
        load.start()
    for load in loads[:6]:
        load.wait()

    high, low = split(f_ref[...])
    pick = pick_ref[...]

    def pack(*parts):
        parts = [dot(pick, values, ((1,), (1,))).reshape(blocks, per, slab) for values in parts]
        return jnp.concatenate(parts, axis=1).astype(BF16)

    packed[...] = pack(k_ref[...], v_ref[...], jnp.concatenate([high, low], axis=1))
    packed_late[...] = pack(q_ref[...], ct_ref[...])

    def remote(number, source, target, pair):
        return pltpu.make_async_remote_copy(
            src_ref=source, dst_ref=target,
            send_sem=send_sems.at[number], recv_sem=recv_sems.at[number], **device(pair),
        )

    def bring(step):
        to = here.member(step)
        remote(0, packed.at[to], held.at[here.seq], here.worker(to, here.chan)).start()

    def bring_late(step):
        to = here.member(step)
        remote(5, packed_late.at[to], held_late.at[here.seq], here.worker(to, here.chan)).start()

    def give(step):
        to = here.member(step)
        remote(1, done.at[to], returned.at[here.work_seq], (to, here.work_chan)).start()

    def give_late(step):
        to = here.member(step)
        remote(6, done_late.at[to], returned_late.at[here.work_seq], (to, here.work_chan)).start()

    def scatter(step):
        to = towards(step)
        place = here.worker(here.work_seq, to)
        remote(2, cross_out.at[here.block(to)], cross_in.at[here.work_chan], place).start()

    def spread(step):
        to = lax.rem(here.chan + 1 + step, count)
        remote(3, total.at[0], shares.at[here.work_seq], (target, to)).start()

    origin = here.worker(here.seq, here.chan)
    pl.semaphore_wait(barrier, blocks + count - 1)
    taps_copy = remote(4, taps_hbm, taps_ref, origin)
    taps_copy.start()
    loop(blocks, bring)
    loop(blocks, bring_late)
    for load in loads[6:]:
        load.wait()
    taps_copy.wait_recv()
    channels = pick.shape[0]
    row = lax.broadcasted_iota(jnp.int32, (per, channels), 0)
    column = lax.broadcasted_iota(jnp.int32, (per, channels), 1)
    wanted = jnp.where(row < per // 2, row, row + (channels - per) // 2) + here.work_seq * (per // 2)
    choice = jnp.where(column == wanted, 1.0, 0.0).astype(F32)
    weights = []
    for p in range(3):
        own = lax.dot_general(
            choice, taps_ref[p], (((1,), (1,)), ((), ())),
            precision=lax.Precision.HIGHEST, preferred_element_type=F32,
        )
        weights.append([own[:, j : j + 1].reshape(1, per, 1) for j in range(own.shape[1])])

    remote(0, packed, held, origin).wait_recv()

    arrived = held[...].astype(F32)
    k, v, filt = (arrived[:, p * per : (p + 1) * per] for p in range(3))
    key_conv = taps(k, weights[1], 1)
    value_conv = taps(v, weights[2], 1)
    gated = (key_conv * value_conv).reshape(blocks * per, slab)
    filt = (filt + pltpu.roll(filt, per // 2, 1)).reshape(blocks * per, slab)

    twist_re, twist_im = twist_re_ref[...], twist_im_ref[...]
    bins = twist_re.shape[0]

    def triple(left_hi, left_lo, right_hi, right_lo):
        return dot(left_hi, right_hi) + (dot(left_hi, right_lo) + dot(left_lo, right_hi))

    def finish(real, imag):
        turned = jnp.concatenate(
            [real * twist_re - imag * twist_im, real * twist_im + imag * twist_re], axis=1
        )
        spec = triple(*split(turned), ahead_hi[...], ahead_lo[...])
        return spec[:, :slab], spec[:, slab:]

    def inverse(real, imag):
        spec = triple(*split(jnp.concatenate([real, imag], axis=1)), back_hi[...], back_lo[...])
        real, imag = spec[:, :slab], spec[:, slab:]
        return jnp.concatenate(
            [real * twist_re + imag * twist_im, imag * twist_re - real * twist_im], axis=0
        )

    def halved(values):
        row = lax.broadcasted_iota(jnp.int32, values.shape, values.ndim - 2)
        high = values.astype(BF16).astype(F32)
        return jnp.where(row < per // 2, high, values - high).astype(BF16)

    def ahead(values):
        both = triple(first_hi[...], first_lo[...], *split(values))
        return [
            finish(both[:bins, at : at + slab], both[bins:, at : at + slab])
            for at in range(0, values.shape[1], slab)
        ]

    def behind(values):
        return triple(last_hi[...], last_lo[...], *split(values)).reshape(blocks, per, slab)

    (g_re, g_im), (f_re, f_im) = ahead(jnp.concatenate([gated, filt], axis=1))
    long_conv = behind(inverse(g_re * f_re - g_im * f_im, g_re * f_im + g_im * f_re))

    remote(5, packed_late, held_late, origin).wait_recv()
    arrived = held_late[...].astype(F32)
    q, incoming = arrived[:, :per], arrived[:, per:]
    query_conv = taps(q, weights[0], 1)
    ((c_re, c_im),) = ahead((incoming * query_conv).reshape(blocks * per, slab))
    cross = behind(inverse(g_re * c_re + g_im * c_im, g_re * c_im - g_im * c_re))
    cross_out[...] = halved(cross + pltpu.roll(cross, per // 2, 1))
    loop(count - 1, scatter)
    kept = pltpu.make_async_copy(cross_out.at[target], cross_in.at[here.work_chan], recv_sems.at[2])
    kept.start()
    parts = [query_conv * long_conv, taps(incoming * long_conv, weights[0], -1)]
    done[...] = jnp.concatenate(parts, axis=1).astype(BF16)
    loop(blocks, give)
    gated_grad = behind(inverse(f_re * c_re + f_im * c_im, f_re * c_im - f_im * c_re))
    parts = [
        taps(gated_grad * value_conv, weights[1], -1),
        taps(gated_grad * key_conv, weights[2], -1),
    ]
    done_late[...] = jnp.concatenate(parts, axis=1).astype(BF16)
    loop(blocks, give_late)

    remote(2, cross_out, cross_in, origin).wait_recv()
    summed = jnp.sum(cross_in[...].astype(F32), axis=0, keepdims=True)
    total[...] = halved(summed + pltpu.roll(summed, per // 2, 1))
    loop(count - 1, spread)

    @pl.when(jnp.logical_not(alone))
    def _():
        spread(jnp.int32(count - 1))
        remote(3, total.at[0], shares.at[0], origin).wait_send()

    @pl.when(alone)
    def _():
        pltpu.make_async_copy(total.at[0], shares.at[here.work_seq], recv_sems.at[3]).start()

    remote(1, done, returned, origin).wait_recv()
    first_out = pltpu.make_async_copy(returned, out_ref.at[:, : 2 * per], load_sems.at[0])
    first_out.start()
    remote(6, done_late, returned_late, origin).wait_recv()
    second_out = pltpu.make_async_copy(returned_late, out_ref.at[:, 2 * per :], load_sems.at[1])
    second_out.start()
    remote(3, shares, shares, origin).wait_recv()
    share_out = pltpu.make_async_copy(shares, share_ref, load_sems.at[2])
    share_out.start()
    taps_copy.wait_send()
    remote(0, packed, held, origin).wait_send()
    remote(1, done, returned, origin).wait_send()
    remote(5, packed_late, held_late, origin).wait_send()
    remote(6, done_late, returned_late, origin).wait_send()
    fewer = pl.ds(0, count - 1)
    remote(2, cross_out.at[fewer], cross_in.at[fewer], origin).wait_send()
    remote(3, shares.at[fewer], shares.at[fewer], origin).wait_send()
    for leaving in (first_out, second_out, share_out):
        leaving.wait()


def call(body, name, outs, *operands, space=pltpu.VMEM, out_space=pltpu.VMEM, **more):
    return pl.pallas_call(
        body,
        name=name,
        out_shape=outs,
        in_specs=[pl.BlockSpec(memory_space=space)] * len(operands),
        out_specs=jax.tree.map(lambda _: pl.BlockSpec(memory_space=out_space), outs),
        **more,
    )(*operands)


def whole(query_rows, key_rows, value_rows, long_filter, cotangent, short_taps):
    slab, channels = query_rows.shape
    blocks = lax.axis_size("seq")
    per = channels // blocks
    pick, _ = orders(blocks, channels)
    shape = functools.partial(jax.ShapeDtypeStruct, dtype=BF16)
    operands = [
        query_rows, key_rows, value_rows, long_filter, cotangent, short_taps, pick,
        *tables(blocks, slab, per),
    ]
    small = pltpu.VMEM((blocks, per, slab), BF16)
    return call(
        whole_kernel,
        "whole",
        [shape((blocks, 4 * per, slab)), shape((blocks, per, slab))],
        *operands,
        space=pl.ANY,
        out_space=pl.ANY,
        scratch_shapes=[
            *[pltpu.VMEM(x.shape, x.dtype) for x in operands],
            *[pltpu.VMEM((blocks, n * per, slab), BF16) for n in (3, 2, 3, 2, 2, 2, 2, 2)],
            small, small, pltpu.VMEM((1, per, slab), BF16), small,
            pltpu.SemaphoreType.DMA((len(operands) - 1,)),
            *[pltpu.SemaphoreType.DMA((7,))] * 2,
        ],
        compiler_params=pltpu.CompilerParams(collective_id=0, has_side_effects=True),
    )


def unpack(returned, shares):
    blocks, per, slab = shares.shape
    channels = blocks * per
    pick, fold = orders(blocks, channels)
    outs = [jax.ShapeDtypeStruct((slab, channels), BF16)] * 4
    outs.append(jax.ShapeDtypeStruct((slab, channels // 2), F32))
    return call(unpack_kernel, "unpack", outs, returned, shares, pick, fold)


def per_device(query_rows, key_rows, value_rows, short_taps, long_filter, cotangent):
    return tuple(
        unpack(*whole(query_rows, key_rows, value_rows, long_filter, cotangent, short_taps))
    )


def solution(mesh):
    wide = P("seq", "chan")
    in_specs = (wide, wide, wide, P(None, None, "chan"), P("seq", None), wide)
    out_specs = (wide, wide, wide, wide, P("seq", None))
    return jax.shard_map(
        per_device, mesh=mesh, in_specs=in_specs, out_specs=out_specs, check_vma=False
    )
```
